32 devices in a mesh: head: 4 (over x, core), tok: 8 (over z, y).
Axes of the slice: x: 2, y: 2, z: 4, core: 2. Of those that a mesh axis runs over, the one named last changes fastest.
Arguments:
- tokens: bfloat16 [512, 4096], P('tok'), may hold values from -6 to 6
- attn_gain: float32 [4096], replicated, may hold values from 0.5 to 1.5
- q_weight: bfloat16 [4096, 2048], P('tok', 'head'), may hold values from -0.09375 to 0.09375
- k_weight: bfloat16 [4096, 512], P('tok', 'head'), may hold values from -0.09375 to 0.09375
- v_weight: bfloat16 [4096, 512], P('tok', 'head'), may hold values from -0.09375 to 0.09375
- output_matrix: bfloat16 [2048, 4096], P('head', 'tok'), may hold values from -0.125 to 0.125
- key_cache: bfloat16 [64, 256, 512], P('tok', None, 'head'), may hold values from -400 to 400
- value_cache: bfloat16 [64, 256, 512], P('tok', None, 'head'), may hold values from -6 to 6
- cache_lengths: int32 [64], P('tok'), may hold values from 1 to 256
- row_request_index: int32 [8, 64], P('tok'), may hold values from 0 to 7, never falling along the last dimension, each value on 1 to 32 neighbouring positions
- ffn_gain: float32 [4096], replicated, may hold values from 0.5 to 1.5
- router_weight: bfloat16 [4096, 8], replicated, may hold values from -0.09375 to 0.09375
- routes: int32 [512, 2], P('tok'), may hold values from 0 to 7, all different within a row; in each aligned block of 64 rows (0 to 63, 64 to 127, ...) at most 18 rows name the same one
- gate_weight: bfloat16 [8, 4096, 14336], P('tok', None, 'head'), may hold values from -0.09375 to 0.09375
- up_weight: bfloat16 [8, 4096, 14336], P('tok', None, 'head'), may hold values from -0.09375 to 0.09375
- down_weight: bfloat16 [8, 14336, 4096], P('tok', None, 'head'), may hold values from -0.046875 to 0.046875
Outputs:
- layer_out: bfloat16 [512, 4096], P('tok', 'head')
The draws below stay inside these ranges and needn't reach their ends.
Inputs may be any that keep to these rules, and one draw needn't show every extreme that they name: `row_request_index`: within the rows of one index of tok the request number never falls, every request has 1 to 32 rows, and one has exactly 32. `routes`: the two experts of a row differ; in the rows of one index of tok no expert is named more than 18 times, and that bound is reached.
All inputs are finite; a program needn't handle non-finite values.
Results may differ from the reference program's by a relative error of at most 0.012.
The reference program's roundings to bfloat16 on the way count: a program that leaves them out, or rounds other values in their place, can miss the bound.
Values may be sent and summed in bfloat16 or wider, within the bound.
A program may use at most 256 MiB of HBM per device.

```python
import math
import jax
import jax.numpy as jnp
import numpy as np
from jax import lax

D = 4096
HD = 128
Q_HEADS = 16
KV_HEADS = 4
FF = 14336
EXPERTS = 8
TOKEN_ROW_SHARE = 64
REQUEST_SHARE = 8
CACHE = 256
MAX_NEW_ROWS = 32
CAP = 18
SLICES = 1
ROWS = 512
REQUESTS = 64
N_TOK = 8


def draw_key_cache(key, part):
    first = jax.random.fold_in(jax.random.fold_in(key, 11), 0)
    values = jnp.clip(jax.random.normal(first, (REQUESTS, CACHE, KV_HEADS * HD), jnp.float32), -5.0, 5.0)
    return values.astype(jnp.bfloat16)


def set_ends(array, key, low, top_value):
    longest = array.shape.index(max(array.shape))
    spots = []
    for shift in (0, 1):
        where = [jax.random.randint(jax.random.fold_in(key, axis), (), 0, length) for axis, length in enumerate(array.shape)]
        where[longest] = (where[longest] + shift) % array.shape[longest]
        spots.append(tuple(where))
    return array.at[spots[0]].set(low).at[spots[1]].set(top_value)


def block_levels(key, extent, cuts, low, largest):
    factor_of = 1.0
    for position, blocks in cuts:
        heights = jax.random.uniform(jax.random.fold_in(jax.random.fold_in(key, 6), position), (blocks,), jnp.float32, low / len(cuts), largest / len(cuts))
        factor_of = factor_of * jnp.repeat(jnp.exp(heights), extent[position] // blocks).reshape((-1,) + (1,) * (len(extent) - 1 - position))
    return factor_of


def profile(count, total, most, slope):
    loads = [(1 << 20) // math.isqrt(rank ** slope) + 1 for rank in range(2, count + 1)]
    rest, given = total - most - (count - 1), [1] * (count - 1)
    while rest > 0:
        free = [i for i in range(count - 1) if given[i] < most]
        mass, remaining = sum([loads[i] for i in free]), rest
        for i in free:
            extra = min(most - given[i], max(1, remaining * loads[i] // mass), rest)
            given[i] = given[i] + extra
            rest = rest - extra
    return np.array([most] + given)


def ragged_sizes(stream_key, number_of, total, bound, slope):
    if number_of == 2:
        one = jax.random.randint(stream_key, (), max(1, total - bound), min(bound, total - 1) + 1)
        return jnp.stack([one, total - one])
    sizes = jnp.asarray(profile(number_of, total, bound, slope), jnp.int32)
    pairs = (number_of - 1) // 2
    source_of, receiver = sizes[1:1 + 2 * pairs:2], sizes[2:2 + 2 * pairs:2]
    room = jnp.minimum(source_of - 1, bound - receiver)
    shifted = jax.random.randint(jax.random.fold_in(stream_key, 1), (pairs,), 0, 1 << 20) % (room + 1)
    sizes = sizes.at[1:1 + 2 * pairs:2].set(source_of - shifted).at[2:2 + 2 * pairs:2].set(receiver + shifted)
    return sizes[jax.random.permutation(jax.random.fold_in(stream_key, 2), number_of)]


def deal_out(own_key, own, number, rows, amount, top, most, slope):
    sequence = jax.random.permutation(own_key, amount)
    heavy_load, common = portions_of(amount, rows * top, most, slope, True), portions_of(amount, rows * top, most, slope, False)
    places = jnp.arange(amount)

    def named(sizes, offset_by):
        used = int((sizes > 0).sum())
        fixed = max(1, used // 4)
        moved = fixed + (places - fixed + offset_by * (used - fixed)) % max(1, amount - fixed)
        return jnp.zeros((amount,), jnp.int32).at[sequence[jnp.where(places < fixed, places, moved)]].set(jnp.asarray(sizes, jnp.int32))

    sizes = jnp.where(number % 4 == 0, named(heavy_load, number // 4), named(common, number - number // 4 - 1))
    mixed = jax.random.permutation(jax.random.fold_in(own, 3), amount)
    giver, sink = mixed[0:amount // 2 * 2:2], mixed[1:amount // 2 * 2:2]
    margin = jnp.minimum(sizes[giver] - 1, most - sizes[sink]) // 2
    margin = jnp.where((giver == sequence[0]) | (sink == sequence[0]) | (sizes[sink] == 0), 0, jnp.maximum(margin, 0))
    moved = jax.random.randint(jax.random.fold_in(own, 4), (amount // 2,), 0, 1 << 20) % (margin + 1)
    sizes = sizes.at[giver].add(-moved).at[sink].add(moved)
    members = jnp.searchsorted(jnp.cumsum(sizes), jnp.arange(rows * top), side="right").astype(jnp.int32)
    listing = members.reshape(top, rows).T
    listing = listing[jax.random.permutation(jax.random.fold_in(own, 1), rows)]
    offset_by = jax.random.randint(jax.random.fold_in(own, 2), (rows, 1), 0, top)
    return jnp.take_along_axis(listing, (jnp.arange(top)[None, :] + offset_by) % top, axis=1)


def portions_of(amount, total, most, lean, full):
    weights = [(1 << 20) // math.isqrt(standing ** lean) + 1 for standing in range(1, amount + 1)]
    largest = most if full else min(most, max(-(-total // amount), total * weights[0] // sum(weights)))
    least = 1 if total - largest >= amount - 1 else 0
    given, surplus = [largest] + [least] * (amount - 1), total - largest - least * (amount - 1)
    while surplus > 0:
        movable = [i for i in range(1, amount) if given[i] < largest] or [i for i in range(1, amount) if given[i] < most]
        pool, remaining = sum([weights[i] for i in movable]), surplus
        for i in movable:
            more = min(most - given[i], max(1, remaining * weights[i] // pool), surplus)
            given[i] = given[i] + more
            surplus = surplus - more
    return np.array(given)


def centred(rng, shape, spread, most, shards=(), kind=jnp.bfloat16):
    array = jax.random.normal(rng, shape, jnp.float32) * spread
    if len(shards) > 0:
        array = block_levels(rng, shape, shards, -0.22, 0.18) * array
    return jnp.clip(array, min=-most, max=most).astype(kind)


def setup_inputs(seed: int = 0) -> dict:
    arg_keys = jax.random.split(jax.random.key(seed), 17)
    tokens = centred(arg_keys[0], (ROWS, D), 1.0, 6.0, ((0, 8),))
    attn_gain = jnp.clip(1.0 + 0.1 * jax.random.normal(arg_keys[1], (D,), jnp.float32), 0.5, 1.5)
    q_weight = centred(arg_keys[2], (D, Q_HEADS * HD), D ** -0.5, 0.09375, ((0, 8), (1, 4)))
    k_weight = centred(arg_keys[3], (D, KV_HEADS * HD), D ** -0.5, 0.09375, ((0, 8), (1, 4)))
    v_weight = centred(arg_keys[4], (D, KV_HEADS * HD), D ** -0.5, 0.09375, ((0, 8), (1, 4)))
    output_matrix = centred(arg_keys[5], (Q_HEADS * HD, D), (Q_HEADS * HD) ** -0.5, 0.125, ((0, 4), (1, 8)))
    key_cache = draw_key_cache(jax.random.fold_in(arg_keys[16], 71), 0)
    value_cache = centred(arg_keys[7], (REQUESTS, CACHE, KV_HEADS * HD), 1.0, 6.0, ((0, 8), (2, 4)))
    cache_lengths = set_ends(jax.random.randint(arg_keys[8], (REQUESTS,), 1, CACHE + 1), jax.random.fold_in(arg_keys[8], 1), 1, CACHE).astype(jnp.int32)
    row_request_index = jax.vmap(lambda own: jnp.searchsorted(jnp.cumsum(ragged_sizes(own, REQUEST_SHARE, TOKEN_ROW_SHARE, MAX_NEW_ROWS, 1)), jnp.arange(TOKEN_ROW_SHARE), side="right"))(jax.random.split(arg_keys[9], N_TOK)).reshape((N_TOK, TOKEN_ROW_SHARE)).astype(jnp.int32)
    ffn_gain = jnp.clip(1.0 + 0.1 * jax.random.normal(arg_keys[10], (D,), jnp.float32), 0.5, 1.5)
    router_weight = centred(arg_keys[11], (D, EXPERTS), D ** -0.5, 0.09375)
    routes_keys = jax.random.split(jax.random.fold_in(arg_keys[12], 1), ROWS // TOKEN_ROW_SHARE)
    routes_turns = jax.random.permutation(jax.random.fold_in(arg_keys[12], 3), ROWS // TOKEN_ROW_SHARE)
    routes = jax.vmap(lambda own, number: deal_out(jax.random.fold_in(arg_keys[12], 2), own, number, TOKEN_ROW_SHARE, EXPERTS, 2, CAP, 2))(routes_keys, routes_turns).reshape((ROWS, 2))
    gate_weight = centred(arg_keys[13], (EXPERTS * SLICES, D, FF // SLICES), D ** -0.5, 0.09375, ((0, 8), (2, 4)))
    up_weight = centred(arg_keys[14], (EXPERTS * SLICES, D, FF // SLICES), D ** -0.5, 0.09375, ((0, 8), (2, 4)))
    down_weight = centred(arg_keys[15], (EXPERTS * SLICES, FF // SLICES, D), FF ** -0.5, 0.046875, ((0, 8), (2, 4)))
    return dict(tokens=tokens, attn_gain=attn_gain, q_weight=q_weight, k_weight=k_weight, v_weight=v_weight, output_matrix=output_matrix, key_cache=key_cache, value_cache=value_cache, cache_lengths=cache_lengths, row_request_index=row_request_index, ffn_gain=ffn_gain, router_weight=router_weight, routes=routes, gate_weight=gate_weight, up_weight=up_weight, down_weight=down_weight)


epsilon = 1e-05
rope_base = 1000000.0

def rms_norm(values, gain):
    values = values.astype(jnp.float32)
    factor = lax.rsqrt(lax.optimization_barrier(jnp.mean(values * values, axis=-1, keepdims=True)) + epsilon)
    return (values * factor * gain.astype(jnp.float32)).astype(jnp.bfloat16)

def rotate(values, positions):
    half = values.shape[-1] // 2
    freqs = rope_base ** (-jnp.arange(half, dtype=jnp.float32) * 2.0 / values.shape[-1])
    angles = positions.astype(jnp.float32)[:, None] * freqs[None, :]
    cosine = jnp.concatenate([jnp.cos(angles), jnp.cos(angles)], axis=-1)[:, None, :]
    sine = jnp.concatenate([jnp.sin(angles), jnp.sin(angles)], axis=-1)[:, None, :]
    turned = jnp.concatenate([-values[..., half:], values[..., :half]], axis=-1)
    return values * cosine + turned * sine

def own_lengths(segment, lengths):
    match = segment[:, None] == jnp.arange(lengths.shape[0], dtype=jnp.int32)[None, :]
    return lax.optimization_barrier(jnp.sum(jnp.where(match, lengths[None, :], 0), axis=1)).astype(jnp.int32)

def row_positions(segment, lengths):
    count = segment.shape[0]
    order = jnp.arange(count, dtype=jnp.int32)
    before = lax.optimization_barrier(jnp.sum((segment[None, :] < segment[:, None]).astype(jnp.int32), axis=1))
    return own_lengths(segment, lengths) + order - before

def attend(queries, new_keys, new_values, key_cache, value_cache, segment, lengths):
    count, kv_local, group, size = queries.shape
    requests, slots, _ = key_cache.shape
    keys = jnp.concatenate([key_cache.reshape(requests * slots, kv_local, size), new_keys], axis=0)
    values = jnp.concatenate([value_cache.reshape(requests * slots, kv_local, size), new_values], axis=0)
    slot_index = jnp.arange(requests * slots, dtype=jnp.int32)
    slot_request = slot_index // slots
    slot_place = slot_index % slots
    limit = own_lengths(segment, lengths)
    cache_valid = (slot_request[None, :] == segment[:, None]) & (slot_place[None, :] < limit[:, None])
    order = jnp.arange(count, dtype=jnp.int32)
    new_valid = (segment[None, :] == segment[:, None]) & (order[None, :] <= order[:, None])
    allowed = jnp.concatenate([cache_valid, new_valid], axis=1)
    scores = jnp.einsum('rhgd,khd->hgrk', queries.astype(jnp.float32), keys.astype(jnp.float32))
    scores = scores / jnp.sqrt(jnp.float32(size))
    scores = jnp.where(allowed[None, None], scores, jnp.float32(-1e+30))
    highest = lax.optimization_barrier(jnp.max(scores, axis=-1, keepdims=True))
    weights = jnp.exp(scores - highest)
    probs = (weights / lax.optimization_barrier(jnp.sum(weights, axis=-1, keepdims=True))).astype(jnp.bfloat16)
    result = jnp.einsum('hgrk,khd->rhgd', probs.astype(jnp.float32), values.astype(jnp.float32))
    return result.astype(jnp.bfloat16).reshape(count, kv_local * group * size)

def slot_table(chosen):
    flat = chosen.reshape(-1).astype(jnp.int32)
    onehot = (flat[:, None] == jnp.arange(EXPERTS, dtype=jnp.int32)[None, :]).astype(jnp.int32)
    earlier = jnp.cumsum(onehot, axis=0) - onehot
    place = lax.optimization_barrier(jnp.sum(earlier * onehot, axis=1))
    return flat * CAP + place

def fill_slots(normed_rows, places):
    copies = normed_rows[jnp.arange(places.shape[0], dtype=jnp.int32) // 2]
    return jnp.zeros((EXPERTS * CAP, normed_rows.shape[1]), jnp.bfloat16).at[places].set(copies)

def gate_shares(normed_rows, router_weight, chosen):
    logits = jnp.dot(normed_rows, router_weight, preferred_element_type=jnp.float32)
    match = chosen[:, :, None] == jnp.arange(EXPERTS, dtype=jnp.int32)[None, None, :]
    picked = lax.optimization_barrier(jnp.sum(jnp.where(match, logits[:, None, :], jnp.float32(0.0)), axis=-1))
    return jax.nn.sigmoid(picked - picked[:, ::-1])

def reference(tokens, attn_gain, q_weight, k_weight, v_weight, output_matrix, key_cache, value_cache, cache_lengths, row_request_index, ffn_gain, router_weight, routes, gate_weight, up_weight, down_weight):
    group = Q_HEADS // KV_HEADS
    normed = rms_norm(tokens, attn_gain)
    queries = jnp.dot(normed, q_weight, preferred_element_type=jnp.float32)
    keys_new = jnp.dot(normed, k_weight, preferred_element_type=jnp.float32)
    values_new = jnp.dot(normed, v_weight, preferred_element_type=jnp.float32)
    lengths_blocks = cache_lengths.reshape(N_TOK, REQUEST_SHARE)
    positions = jax.vmap(row_positions)(row_request_index, lengths_blocks).reshape(-1)
    queries = rotate(queries.reshape(ROWS, Q_HEADS, HD), positions).astype(jnp.bfloat16)
    keys_new = rotate(keys_new.reshape(ROWS, KV_HEADS, HD), positions).astype(jnp.bfloat16)
    values_new = values_new.astype(jnp.bfloat16)

    def one_block(pieces):
        q_block, k_block, v_block, k_store, v_store, segment, lengths = pieces
        return attend(q_block.reshape(TOKEN_ROW_SHARE, KV_HEADS, group, HD), k_block, v_block.reshape(TOKEN_ROW_SHARE, KV_HEADS, HD), k_store, v_store, segment, lengths)
    attn = lax.map(one_block, (queries.reshape(N_TOK, TOKEN_ROW_SHARE, Q_HEADS, HD), keys_new.reshape(N_TOK, TOKEN_ROW_SHARE, KV_HEADS, HD), values_new.reshape(N_TOK, TOKEN_ROW_SHARE, KV_HEADS * HD), key_cache.reshape(N_TOK, REQUEST_SHARE, CACHE, KV_HEADS * HD), value_cache.reshape(N_TOK, REQUEST_SHARE, CACHE, KV_HEADS * HD), row_request_index, lengths_blocks))
    attn = attn.reshape(ROWS, Q_HEADS * HD)
    hidden_activation = tokens.astype(jnp.float32) + jnp.dot(attn, output_matrix, preferred_element_type=jnp.float32)
    normed_ffn = rms_norm(hidden_activation, ffn_gain)
    shares = gate_shares(normed_ffn, router_weight, routes)
    places = jax.vmap(slot_table)(routes.reshape(N_TOK, TOKEN_ROW_SHARE, 2))
    buffers = jax.vmap(fill_slots)(normed_ffn.reshape(N_TOK, TOKEN_ROW_SHARE, D), places)
    buffers = buffers.reshape(N_TOK, EXPERTS, CAP, D).transpose(1, 0, 2, 3).reshape(EXPERTS, N_TOK * CAP, D)
    width = FF // SLICES
    gate_pieces_list = gate_weight.reshape(EXPERTS, SLICES, D, width)
    up_parts = up_weight.reshape(EXPERTS, SLICES, D, width)
    down_parts = down_weight.reshape(EXPERTS, SLICES, width, D)

    def expert(pieces):
        slot_rows, gates, ups, downs = pieces

        def add_block(total, weights):
            gate_block, up_block, down_block = weights
            active = jnp.dot(slot_rows, gate_block, preferred_element_type=jnp.float32)
            linear = jnp.dot(slot_rows, up_block, preferred_element_type=jnp.float32)
            hidden = (jax.nn.silu(active) * linear).astype(jnp.bfloat16)
            output = jnp.dot(hidden, down_block, preferred_element_type=jnp.float32).astype(jnp.bfloat16)
            output = lax.optimization_barrier(output)
            return (total + output.astype(jnp.float32), None)
        total, _ = lax.scan(add_block, jnp.zeros((slot_rows.shape[0], D), jnp.float32), (gates, ups, downs))
        return total
    outputs = lax.map(expert, (buffers, gate_pieces_list, up_parts, down_parts))
    flat_out = outputs.reshape(EXPERTS * N_TOK * CAP, D)
    expert_ids = places // CAP
    slot_ids = places % CAP
    block_ids = jnp.arange(N_TOK, dtype=jnp.int32)[:, None]
    global_ids = (expert_ids * (N_TOK * CAP) + block_ids * CAP + slot_ids).reshape(-1)
    picked = jnp.take(flat_out, global_ids, axis=0).reshape(ROWS, 2, D)
    mixture = lax.optimization_barrier(jnp.sum(shares[:, :, None] * picked, axis=1))
    return (hidden_activation + mixture).astype(jnp.bfloat16)
```

```python
import functools

import jax
import jax.numpy as jnp
import numpy as np
from jax import lax
from jax.experimental import pallas as pl
from jax.experimental.pallas import tpu as pltpu
from jax.sharding import PartitionSpec as P

D = 4096
HD = 128
Q_HEADS = 16
KV_HEADS = 4
EXPERTS = 8
CAP = 18


epsilon = 1e-05
rope_base = 1000000.0


def rms_norm(values, gain):
    values = values.astype(jnp.float32)
    factor = lax.rsqrt(jnp.mean(values * values, axis=-1, keepdims=True) + epsilon)
    return (values * factor * gain).astype(jnp.bfloat16)


def rotate(values, positions):
    half = values.shape[-1] // 2
    freqs = rope_base ** (-jnp.arange(half, dtype=jnp.float32) * 2.0 / values.shape[-1])
    angles = positions.astype(jnp.float32)[:, None] * freqs[None, :]
    cosine = jnp.concatenate([jnp.cos(angles), jnp.cos(angles)], axis=-1)[:, None, :]
    sine = jnp.concatenate([jnp.sin(angles), jnp.sin(angles)], axis=-1)[:, None, :]
    turned = jnp.concatenate([-values[..., half:], values[..., :half]], axis=-1)
    return values * cosine + turned * sine


def own_lengths(segment, lengths):
    match = segment[:, None] == jnp.arange(lengths.shape[0], dtype=jnp.int32)[None, :]
    return jnp.sum(jnp.where(match, lengths[None, :], 0), axis=1)


def row_positions(segment, lengths):
    count = segment.shape[0]
    order = jnp.arange(count, dtype=jnp.int32)
    before = jnp.sum((segment[None, :] < segment[:, None]).astype(jnp.int32), axis=1)
    return own_lengths(segment, lengths) + order - before


def attend(queries, new_keys, new_values, key_cache, value_cache, segment, lengths):
    count, kv_local, group, size = queries.shape
    requests, slots, _ = key_cache.shape
    keys = jnp.concatenate([key_cache.reshape(requests * slots, kv_local, size), new_keys], axis=0)
    values = jnp.concatenate(
        [value_cache.reshape(requests * slots, kv_local, size), new_values], axis=0
    )
    slot_index = jnp.arange(requests * slots, dtype=jnp.int32)
    slot_request = slot_index // slots
    slot_place = slot_index % slots
    limit = own_lengths(segment, lengths)
    cache_valid = (slot_request[None, :] == segment[:, None]) & (
        slot_place[None, :] < limit[:, None]
    )
    order = jnp.arange(count, dtype=jnp.int32)
    new_valid = (segment[None, :] == segment[:, None]) & (order[None, :] <= order[:, None])
    allowed = jnp.concatenate([cache_valid, new_valid], axis=1)
    scores = jnp.einsum("rhgd,khd->hgrk", queries, keys, preferred_element_type=jnp.float32)
    scores = scores / jnp.sqrt(jnp.float32(size))
    scores = jnp.where(allowed[None, None], scores, jnp.float32(-1e30))
    highest = jnp.max(scores, axis=-1, keepdims=True)
    weights = jnp.exp(scores - highest)
    probs = (weights / jnp.sum(weights, axis=-1, keepdims=True)).astype(jnp.bfloat16)
    result = jnp.einsum("hgrk,khd->rhgd", probs, values, preferred_element_type=jnp.float32)
    return result.astype(jnp.bfloat16).reshape(count, kv_local * group * size)


def slot_table(chosen):
    flat = chosen.reshape(-1)
    onehot = (flat[:, None] == jnp.arange(EXPERTS, dtype=jnp.int32)[None, :]).astype(jnp.int32)
    earlier = jnp.cumsum(onehot, axis=0) - onehot
    place = jnp.sum(earlier * onehot, axis=1)
    return flat * CAP + place


def fill_slots(normed_rows, places):
    copies = normed_rows[jnp.arange(places.shape[0], dtype=jnp.int32) // 2]
    return jnp.zeros((EXPERTS * CAP, normed_rows.shape[1]), jnp.bfloat16).at[places].set(copies)


def gate_shares(normed_rows, router_weight, chosen):
    logits = jnp.dot(normed_rows, router_weight, preferred_element_type=jnp.float32)
    match = chosen[:, :, None] == jnp.arange(EXPERTS, dtype=jnp.int32)[None, None, :]
    picked = jnp.sum(jnp.where(match, logits[:, None, :], jnp.float32(0.0)), axis=-1)
    return jax.nn.sigmoid(picked - picked[:, ::-1])


def shards(
    tokens,
    attn_gain,
    q_weight,
    k_weight,
    v_weight,
    output_matrix,
    key_cache,
    value_cache,
    cache_lengths,
    row_request_index,
    ffn_gain,
    router_weight,
    routes,
    gate_weight,
    up_weight,
    down_weight,
):
    count = tokens.shape[0]
    group = Q_HEADS // KV_HEADS
    normed = rms_norm(tokens, attn_gain)
    q_full, k_full, v_full, o_full = (
        lax.all_gather(q_weight, "tok", axis=0, tiled=True),
        lax.all_gather(k_weight, "tok", axis=0, tiled=True),
        lax.all_gather(v_weight, "tok", axis=0, tiled=True),
        lax.all_gather(output_matrix, "tok", axis=1, tiled=True),
    )
    kv_local = k_full.shape[1] // HD
    queries = jnp.dot(normed, q_full, preferred_element_type=jnp.float32)
    keys_new = jnp.dot(normed, k_full, preferred_element_type=jnp.float32)
    values_new = jnp.dot(normed, v_full, preferred_element_type=jnp.float32)
    segment = row_request_index[0]
    positions = row_positions(segment, cache_lengths)
    queries = rotate(queries.reshape(count, kv_local * group, HD), positions).astype(jnp.bfloat16)
    queries = queries.reshape(count, kv_local, group, HD)
    keys_new = rotate(keys_new.reshape(count, kv_local, HD), positions).astype(jnp.bfloat16)
    values_new = values_new.astype(jnp.bfloat16).reshape(count, kv_local, HD)
    attn = attend(queries, keys_new, values_new, key_cache, value_cache, segment, cache_lengths)
    partial_mix = jnp.dot(attn, o_full, preferred_element_type=jnp.float32)
    mixed = lax.psum(partial_mix, "head")
    hidden_activation = tokens.astype(jnp.float32) + mixed
    normed_ffn = rms_norm(hidden_activation, ffn_gain)
    shares = gate_shares(normed_ffn, router_weight, routes)
    places = slot_table(routes)
    buffer = fill_slots(normed_ffn, places)
    owners = lax.axis_size("tok")
    slices = owners // EXPERTS
    quarter = down_weight.shape[2]
    head_index = lax.axis_index("head")
    outgoing = jnp.broadcast_to(
        buffer.reshape(EXPERTS, 1, CAP, D), (EXPERTS, slices, CAP, D)
    ).reshape(owners, CAP, D)
    arrived = lax.all_to_all(outgoing, "tok", split_axis=0, concat_axis=0, tiled=True)
    active = jnp.einsum("tcd,df->tcf", arrived, gate_weight[0], preferred_element_type=jnp.float32)
    linear = jnp.einsum("tcd,df->tcf", arrived, up_weight[0], preferred_element_type=jnp.float32)
    hidden = (jax.nn.silu(active) * linear).astype(jnp.bfloat16)
    hidden_all = lax.all_gather(hidden, "head", axis=2, tiled=True)
    output = jnp.einsum(
        "tcf,fd->tcd", hidden_all, down_weight[0], preferred_element_type=jnp.float32
    )
    layer_results = output.astype(jnp.bfloat16)
    returned = lax.all_to_all(layer_results, "tok", split_axis=0, concat_axis=0, tiled=True)
    summed = jnp.sum(returned.reshape(EXPERTS, slices, CAP, quarter).astype(jnp.float32), axis=1)
    summed = summed.reshape(EXPERTS * CAP, quarter)
    picked = jnp.take(summed, places, axis=0).reshape(count, 2, quarter)
    mixture = jnp.sum(shares[:, :, None] * picked, axis=1)
    residual = lax.dynamic_slice_in_dim(hidden_activation, head_index * quarter, quarter, 1)
    return (residual + mixture).astype(jnp.bfloat16)


MESH = pl.DeviceIdType.MESH
F32 = jnp.float32
BF16 = jnp.bfloat16
MAIN = 16
NW = 3
ND = 12
FC = 512


def rcopy(src, dst, send_sem, recv_sem, head, tok):
    return pltpu.make_async_remote_copy(
        src_ref=src, dst_ref=dst, send_sem=send_sem, recv_sem=recv_sem,
        device_id={"head": head, "tok": tok}, device_id_type=MESH,
    )


def mm(a, b):
    return jnp.dot(a, b, preferred_element_type=F32)


def relatives(head):
    core, side = lax.rem(head, 2), head // 2
    return head, side * 2 + 1 - core, (1 - side) * 2 + core, (1 - side) * 2 + 1 - core


def ahead(me, n, s):
    return lax.rem(me // 2 + s // 2, n // 2) * 2 + (lax.rem(me + s % 2, 2))


def behind(me, n, s):
    return lax.rem(me // 2 + n // 2 - s // 2, n // 2) * 2 + (lax.rem(me + s % 2, 2))


def project_kernel(n, m, tok_ref, gain_ref, q_ref, k_ref, v_ref, out_ref,
                   nrm, xin, keep, parta, pa, partb, pb, s1, r1, s3, r3, s2, r2, s4, r4):
    me = lax.axis_index("tok")
    head = lax.axis_index("head")
    heads = relatives(head)
    barrier = pltpu.get_barrier_semaphore()
    for d in range(1, n):
        pl.semaphore_signal(barrier, inc=1, device_id={"head": head, "tok": lax.rem(me + d, n)},
                            device_id_type=MESH)
    for i in range(1, m):
        pl.semaphore_signal(barrier, inc=1, device_id={"head": heads[i], "tok": me},
                            device_id_type=MESH)
    values = tok_ref[...].astype(F32)
    factor = lax.rsqrt(jnp.mean(values * values, axis=-1, keepdims=True) + epsilon)
    normed = (values * factor * gain_ref[...]).astype(BF16)
    width = normed.shape[1] // n
    for j in range(n):
        nrm[j] = normed[:, j * width:(j + 1) * width]
    pl.semaphore_wait(barrier, n + m - 2)
    share_rows = normed.shape[0] // m

    def rows(h):
        return pl.ds(pl.multiple_of(h * share_rows, share_rows), share_rows)

    def first(s):
        to = ahead(me, n, s)
        return rcopy(nrm.at[to, rows(head)], xin.at[s, rows(head)], s1.at[s], r1.at[s], head, to)

    def share(s, i):
        part = xin.at[s, rows(head)]
        return rcopy(part, part, s3.at[s, i], r3.at[s, i], heads[i], me)

    def shared(s, i):
        part = xin.at[s, rows(heads[i])]
        return rcopy(part, part, s3.at[s, i], r3.at[s, i], heads[i], me)

    def across(z):
        return rcopy(parta.at[z], pa.at[z], s2.at[z], r2.at[z], head, ahead(me, n, 1))

    def along(z):
        return rcopy(partb.at[z], pb.at[z], s4.at[z], r4.at[z], head, behind(me, n, 2 * z))

    def project(x):
        return jnp.concatenate([mm(x, q_ref[...]), mm(x, k_ref[...]), mm(x, v_ref[...])], axis=1)

    order = [3, 2, 5, 4, 7, 6, 1]
    for s in order:
        first(s).start()
    keep[0] = project(nrm[me])
    for s in order:
        first(s).wait_recv()
        for i in (2, 3, 1):
            share(s, i).start()

    def pass_on(z):
        across(z).wait_recv()
        if z == 0:
            keep[0] += pa[0].astype(F32)
        else:
            partb[z] = (keep[z] + pa[z].astype(F32)).astype(BF16)
            along(z).start()

    for s in order:
        for i in range(1, m):
            shared(s, i).wait_recv()
        z = s // 2
        if s % 2:
            parta[z] = project(xin[s]).astype(BF16)
            across(z).start()
            if z == 0:
                pass_on(n // 2 - 1)
                pass_on(0)
        else:
            keep[z] = project(xin[s])
            if z > 1:
                pass_on(z - 1)
    total = keep[0]
    for z in range(1, n // 2):
        along(z).wait_recv()
        total = total + pb[z].astype(F32)
    out_ref[...] = total
    for s in order:
        first(s).wait_send()
        for i in range(1, m):
            share(s, i).wait_send()
    for z in range(n // 2):
        across(z).wait_send()
        if z > 0:
            along(z).wait_send()


def project(n, m, tokens, gain, q_weight, k_weight, v_weight):
    rows, width = tokens.shape
    cols = q_weight.shape[1] + k_weight.shape[1] + v_weight.shape[1]
    dma = pltpu.SemaphoreType.DMA
    return pl.pallas_call(
        functools.partial(project_kernel, n, m),
        out_shape=jax.ShapeDtypeStruct((rows, cols), F32),
        in_specs=[pl.BlockSpec(memory_space=pltpu.VMEM)] * 5,
        out_specs=pl.BlockSpec(memory_space=pltpu.VMEM),
        scratch_shapes=[
            pltpu.VMEM((n, rows, width // n), BF16),
            pltpu.VMEM((n, rows, width // n), BF16),
            pltpu.VMEM((n // 2, rows, cols), F32),
            pltpu.VMEM((n // 2, rows, cols), BF16),
            pltpu.VMEM((n // 2, rows, cols), BF16),
            pltpu.VMEM((n // 2, rows, cols), BF16),
            pltpu.VMEM((n // 2, rows, cols), BF16),
            dma((n,)), dma((n,)), dma((n, m)), dma((n, m)),
            dma((n // 2,)), dma((n // 2,)), dma((n // 2,)), dma((n // 2,)),
        ],
        compiler_params=pltpu.CompilerParams(collective_id=0, has_side_effects=True),
    )(tokens, gain.reshape(1, -1), q_weight, k_weight, v_weight)


def experts_kernel(n, m, attn_ref, w_ref, tok_ref, gain_ref, router_ref, pmain_ref, ptail_ref,
                   sel_ref, seltail_ref, fold_ref, unfold_ref, chosen_ref, gate_ref, up_ref, down_ref,
                   out_ref,
                   ain, part, pin, stat, logit, xs, xin, xall, gbuf, ubuf, hall, dbuf, acc, yout, yin,
                   hid_ref,
                   sa, ra, sp, rp, ss, rs, sl, rl, sx, rx, sg, rg, sh, rh, sy, ry, gsem, usem, dsem):
    me = lax.axis_index("tok")
    head = lax.axis_index("head")
    heads = relatives(head)
    sib = heads[1]
    steps = gate_ref.shape[2] // FC
    local = gate_ref.shape[2]
    quarter = tok_ref.shape[1]
    total = n * m
    flat = head * n + me
    barrier = pltpu.get_barrier_semaphore()

    @pl.loop(1, total)
    def _(d):
        other = lax.rem(flat + d, total)
        pl.semaphore_signal(barrier, inc=1, device_id={"head": other // n, "tok": lax.rem(other, n)},
                            device_id_type=MESH)

    def wcopies(j, slot):
        cols = pl.ds(pl.multiple_of(j * FC, FC), FC)
        return (pltpu.make_async_copy(gate_ref.at[0, :, cols], gbuf.at[slot], gsem.at[slot]),
                pltpu.make_async_copy(up_ref.at[0, :, cols], ubuf.at[slot], usem.at[slot]))

    def dcopy(r, j, slot):
        which = heads[0]
        for i in range(1, m):
            which = jnp.where(r == i, heads[i], which)
        start = pl.multiple_of(which * local + j * FC, FC)
        return pltpu.make_async_copy(down_ref.at[0, pl.ds(start, FC), :], dbuf.at[slot], dsem.at[slot])

    for j in range(NW):
        for c in wcopies(j, j):
            c.start()
    for k in range(ND):
        dcopy(k // steps, k % steps, k).start()
    pl.semaphore_wait(barrier, total - 1)

    group = n // m
    target = me // group
    myslot = head * group + lax.rem(me, group)

    def acopy(s):
        if s > 1 and s % 2:
            return rcopy(ain.at[s - 1], ain.at[s], sa.at[s], ra.at[s], head, ahead(me, n, 1))
        return rcopy(attn_ref, ain.at[s], sa.at[s], ra.at[s], head, ahead(me, n, s))

    def pcopy(s):
        return rcopy(part.at[s], pin.at[myslot], sp.at[s], rp.at[myslot], target, behind(me, n, s))

    for s in [*range(2, n, 2), 1]:
        acopy(s).start()
    own = mm(attn_ref[...], w_ref[...]).astype(BF16)
    mine = head == target

    @pl.when(mine)
    def _():
        pin[myslot] = own

    @pl.when(jnp.logical_not(mine))
    def _():
        part[0] = own
        pcopy(0).start()

    def mixed(s):
        part[s] = mm(ain[s], w_ref[...]).astype(BF16)
        pcopy(s).start()

    acopy(1).wait_recv()
    mixed(1)
    for s in range(2, n, 2):
        acopy(s).wait_recv()
        acopy(s + 1).start()
        mixed(s)
        if s > 2:
            acopy(s - 1).wait_recv()
            mixed(s - 1)
    acopy(n - 1).wait_recv()
    mixed(n - 1)
    for s in range(m * group):
        @pl.when(jnp.logical_not(mine & (myslot == s)))
        def _():
            rcopy(part.at[0], pin.at[s], sp.at[0], rp.at[s], sib, me).wait_recv()
    hidden = tok_ref[...].astype(F32)
    sums = []
    for g in range(group):
        t = pin[g].astype(F32)
        for h in range(1, m):
            t = t + pin[h * group + g].astype(F32)
        sums.append(t)
    hidden = hidden + jnp.concatenate(sums, axis=1)
    hid_ref[...] = hidden

    def exchange(buf, ssem, rsem, i):
        return rcopy(buf.at[0], buf.at[i], ssem.at[i], rsem.at[i], heads[i], me)

    stat[0] = jnp.broadcast_to(jnp.sum(hidden * hidden, axis=-1, keepdims=True), stat.shape[1:])
    for i in range(1, m):
        exchange(stat, ss, rs, i).start()
    for i in range(1, m):
        exchange(stat, ss, rs, i).wait_recv()
    square = stat[0]
    for i in range(1, m):
        square = square + stat[i]
    factor = lax.rsqrt(square[:, :1] / (quarter * m) + epsilon)
    normed = (hidden * factor * gain_ref[...]).astype(BF16)

    main = mm(pmain_ref[...], normed).astype(BF16)
    chunks = quarter // 128
    tail = mm(ptail_ref[0], normed[:, :128])
    for c in range(1, chunks):
        tail = tail + mm(ptail_ref[c], normed[:, c * 128:(c + 1) * 128])
    tail = tail.astype(BF16)
    for e in range(n):
        xs[e, :, :quarter] = main[e * MAIN:(e + 1) * MAIN]
        xs[e, :, quarter:] = tail[e * MAIN:(e + 1) * MAIN]

    def xcopy(d):
        to = lax.rem(me + d, n)
        return rcopy(xs.at[to], xin.at[d], sx.at[d], rx.at[d], head, to)

    for d in range(1, n):
        xcopy(d).start()
    xin[0] = xs[me]
    logit[0] = mm(normed, router_ref[...])
    for i in range(1, m):
        exchange(logit, sl, rl, i).start()
    for d in range(1, n):
        xcopy(d).wait_recv()
    for d in range(n):
        xall[0, d * MAIN:(d + 1) * MAIN] = xin[d, :, :quarter]
    tails = jnp.concatenate([xin[d, :, quarter:] for d in range(n)], axis=0)
    for c in range(chunks):
        xall[0, n * MAIN:, c * 128:(c + 1) * 128] = mm(fold_ref[c], tails).astype(BF16)

    def gcopy(i):
        if i == 3:
            return rcopy(xall.at[2], xall.at[3], sg.at[3], rg.at[3], sib, me)
        return rcopy(xall.at[0], xall.at[i], sg.at[i], rg.at[i], heads[i], me)

    gcopy(2).start()
    gcopy(1).start()
    gcopy(2).wait_recv()
    gcopy(3).start()
    gcopy(1).wait_recv()
    gcopy(3).wait_recv()

    def hcopy(i, j):
        if i == 3:
            return rcopy(hall.at[2, j], hall.at[3, j], sh.at[3, j], rh.at[3, j], sib, me)
        return rcopy(hall.at[0, j], hall.at[i, j], sh.at[i, j], rh.at[i, j], heads[i], me)

    lag = 2

    def forward(j):
        hcopy(2, j).wait_recv()
        hcopy(3, j).start()

    @pl.loop(0, steps)
    def _(j):
        slot = lax.rem(j, NW)
        for c in wcopies(j, slot):
            c.wait()
        g = jnp.zeros((xall.shape[1], FC), F32)
        u = jnp.zeros((xall.shape[1], FC), F32)
        for i in range(m):
            rows = pl.ds(pl.multiple_of(heads[i] * quarter, quarter), quarter)
            g = g + mm(xall[i], gbuf[slot, rows, :])
            u = u + mm(xall[i], ubuf[slot, rows, :])
        hall[0, j] = ((g / (1.0 + jnp.exp(-g))) * u).astype(BF16)
        hcopy(2, j).start()
        hcopy(1, j).start()

        @pl.when(j + NW < steps)
        def _():
            for c in wcopies(j + NW, slot):
                c.start()

        @pl.when(j >= lag)
        def _():
            forward(j - lag)

    acc[...] = jnp.zeros_like(acc)

    def segment(r):
        @pl.loop(0, steps)
        def _(j):
            k = r * steps + j
            slot = lax.rem(k, ND)
            if r in (1, 3):
                hcopy(r, j).wait_recv()
            dcopy(r, j, slot).wait()
            acc[...] += mm(hall[r, j], dbuf[slot])

            @pl.when(k + ND < m * steps)
            def _():
                dcopy((k + ND) // steps, lax.rem(k + ND, steps), slot).start()

    segment(0)
    forward(steps - 2)
    segment(1)
    forward(steps - 1)
    segment(2)
    segment(3)

    result = acc[...].astype(BF16)
    rest = result[n * MAIN:]
    back = mm(unfold_ref[0], rest[:, :128])
    for c in range(1, chunks):
        back = back + mm(unfold_ref[c], rest[:, c * 128:(c + 1) * 128])
    back = back.astype(BF16)

    def ycopy(d):
        return rcopy(yout.at[d], yin.at[me], sy.at[d], ry.at[d], head, lax.rem(me + n - d, n))

    for d in range(n):
        yout[d, :, :quarter] = result[d * MAIN:(d + 1) * MAIN]
        yout[d, :, quarter:] = back[d * MAIN:(d + 1) * MAIN]
        if d > 0:
            ycopy(d).start()
    yin[me] = yout[0]

    for i in range(1, m):
        exchange(logit, sl, rl, i).wait_recv()
    logits = logit[0]
    for i in range(1, m):
        logits = logits + logit[i]
    lane = lax.broadcasted_iota(jnp.int32, logits.shape, 1)
    picks = [jnp.sum(jnp.where(lane == chosen_ref[:, k:k + 1], logits, 0.0), axis=-1, keepdims=True)
             for k in range(2)]
    shares = [jax.nn.sigmoid(picks[0] - picks[1]), jax.nn.sigmoid(picks[1] - picks[0])]

    for d in range(1, n):
        rcopy(yout.at[d], yin.at[lax.rem(me + d, n)], sy.at[d], ry.at[d], head, me).wait_recv()
    mains = jnp.concatenate([yin[e, :, :quarter] for e in range(n)], axis=0)
    ends = jnp.concatenate([yin[e, :, quarter:] for e in range(n)], axis=0)
    mixture = None
    for k in range(2):
        wide = jnp.concatenate([mm(seltail_ref[k * chunks + c], ends) for c in range(chunks)], axis=1)
        term = shares[k] * (mm(sel_ref[k], mains) + wide)
        mixture = term if mixture is None else mixture + term
    out_ref[...] = (hid_ref[...] + mixture).astype(BF16)

    for d in range(1, n):
        acopy(d).wait_send()
        pcopy(d).wait_send()
        xcopy(d).wait_send()
        ycopy(d).wait_send()

    @pl.when(jnp.logical_not(mine))
    def _():
        pcopy(0).wait_send()

    for i in range(1, m):
        exchange(stat, ss, rs, i).wait_send()
        exchange(logit, sl, rl, i).wait_send()
        gcopy(i).wait_send()

        @pl.loop(0, steps)
        def _(j):
            hcopy(i, j).wait_send()


def experts(n, m, attn, weight, tokens, gain, router, tables, chosen, gate, up, down):
    rows, quarter = tokens.shape
    deep, wide = weight.shape
    slots = n * CAP
    steps = gate.shape[2] // FC
    dma = pltpu.SemaphoreType.DMA
    vm = pl.BlockSpec(memory_space=pltpu.VMEM)
    hbm = pl.BlockSpec(memory_space=pltpu.HBM)
    return pl.pallas_call(
        functools.partial(experts_kernel, n, m),
        out_shape=jax.ShapeDtypeStruct((rows, quarter), BF16),
        in_specs=[vm] * 12 + [hbm] * 3,
        out_specs=vm,
        scratch_shapes=[
            pltpu.VMEM((n, rows, deep), BF16),
            pltpu.VMEM((n, rows, wide), BF16),
            pltpu.VMEM((n, rows, wide), BF16),
            pltpu.VMEM((m, rows, 128), F32),
            pltpu.VMEM((m, rows, 128), F32),
            pltpu.VMEM((n, MAIN, quarter + 128), BF16),
            pltpu.VMEM((n, MAIN, quarter + 128), BF16),
            pltpu.VMEM((m, slots, quarter), BF16),
            pltpu.VMEM((NW, gate.shape[1], FC), BF16),
            pltpu.VMEM((NW, gate.shape[1], FC), BF16),
            pltpu.VMEM((m, steps, slots, FC), BF16),
            pltpu.VMEM((ND, FC, quarter), BF16),
            pltpu.VMEM((slots, quarter), F32),
            pltpu.VMEM((n, MAIN, quarter + 128), BF16),
            pltpu.VMEM((n, MAIN, quarter + 128), BF16),
            pltpu.VMEM((rows, quarter), F32),
            dma((n,)), dma((n,)), dma((n,)), dma((n,)),
            dma((m,)), dma((m,)), dma((m,)), dma((m,)),
            dma((n,)), dma((n,)), dma((m,)), dma((m,)),
            dma((m, steps)), dma((m, steps)), dma((n,)), dma((n,)),
            dma((NW,)), dma((NW,)), dma((ND,)),
        ],
        compiler_params=pltpu.CompilerParams(
            collective_id=1, has_side_effects=True, vmem_limit_bytes=60 * 1024 * 1024),
    )(attn, weight, tokens, gain, router, *tables, chosen, gate, up, down)


def slot_tables(chosen, chunks):
    places = slot_table(chosen).reshape(chosen.shape)
    slot = places - chosen * CAP
    more = CAP - MAIN
    where = jnp.arange(EXPERTS * MAIN, dtype=jnp.int32)
    expert, place = where // MAIN, where % MAIN
    match = chosen[:, :, None] == expert
    sel = match & (slot[:, :, None] == place)
    chunk = jnp.arange(chunks, dtype=jnp.int32)[:, None]
    end = (place // more == chunk) & (place % more >= 0)
    seltail = (match & (slot[:, :, None] == MAIN + place % more))[:, :, None, :] & end
    sel = sel.transpose(1, 0, 2)
    seltail = seltail.transpose(1, 2, 0, 3)
    pmain = (sel[0] | sel[1]).T
    ptail = (seltail[0] | seltail[1]).transpose(0, 2, 1)
    group = np.arange(EXPERTS * more)
    spot = np.arange(EXPERTS * MAIN)
    fold = (group[:, None] // more == spot // MAIN) & (group[:, None] % more == spot % more)
    fold = fold[None] & (spot % MAIN // more == np.arange(chunks)[:, None])[:, None, :]
    unfold = fold.transpose(0, 2, 1)
    seltail = seltail.reshape(2 * chunks, chosen.shape[0], -1)
    return [jnp.asarray(a, BF16) for a in (pmain, ptail, sel, seltail, fold, unfold)]


def shards_eight(
    tokens, attn_gain, q_weight, k_weight, v_weight, output_matrix, key_cache, value_cache,
    cache_lengths, row_request_index, ffn_gain, router_weight, routes, gate_weight, up_weight,
    down_weight,
):
    count = tokens.shape[0]
    group = Q_HEADS // KV_HEADS
    n, m = lax.axis_size("tok"), lax.axis_size("head")
    head_index = lax.axis_index("head")
    quarter = down_weight.shape[2]
    tables = slot_tables(routes, quarter // 128)
    qkv = project(n, m, tokens, attn_gain, q_weight, k_weight, v_weight)
    qw, kw = q_weight.shape[1], k_weight.shape[1]
    kv_local = kw // HD
    segment = row_request_index[0]
    positions = row_positions(segment, cache_lengths)
    queries = rotate(qkv[:, :qw].reshape(count, kv_local * group, HD), positions).astype(BF16)
    queries = queries.reshape(count, kv_local, group, HD)
    keys_new = rotate(qkv[:, qw:qw + kw].reshape(count, kv_local, HD), positions).astype(BF16)
    values_new = qkv[:, qw + kw:].astype(BF16).reshape(count, kv_local, HD)
    attn = attend(queries, keys_new, values_new, key_cache, value_cache, segment, cache_lengths)
    cut = functools.partial(lax.dynamic_slice_in_dim, start_index=head_index * quarter, slice_size=quarter)
    router = jnp.pad(cut(router_weight, axis=0), ((0, 0), (0, 128 - EXPERTS)))
    return experts(
        n, m, attn, output_matrix, cut(tokens, axis=1), cut(ffn_gain, axis=0).reshape(1, -1), router,
        tables, routes, gate_weight, up_weight, down_weight,
    )


def solution(mesh):
    in_specs = (
        P("tok", None),
        P(),
        P("tok", "head"),
        P("tok", "head"),
        P("tok", "head"),
        P("head", "tok"),
        P("tok", None, "head"),
        P("tok", None, "head"),
        P("tok"),
        P("tok", None),
        P(),
        P(),
        P("tok", None),
        P("tok", None, "head"),
        P("tok", None, "head"),
        P("tok", None, "head"),
    )
    out_specs = P("tok", "head")
    body = shards_eight if mesh.shape["tok"] == EXPERTS and mesh.shape["head"] == KV_HEADS else shards
    return jax.shard_map(body, mesh=mesh, in_specs=in_specs, out_specs=out_specs, check_vma=False)
```
